32 devices in a mesh: dp: 4 (over z), row: 4 (over y, x), col: 2 (over core).
Axes of the slice: x: 2, y: 2, z: 4, core: 2. Of those that a mesh axis runs over, the one named last changes fastest.
Arguments:
- hidden_in: bfloat16 [32768, 768], P(('dp', 'row'), 'col'), may hold values from -6 to 6
- doc_ids: int32 [16, 2048], P(('dp', 'row')), may hold values from 0 to 3, never falling along the last dimension, each value on 1 to 1024 neighbouring positions
- norm_gain: bfloat16 [768], P('col'), may hold values from 0.5 to 1.5
- proj_gate: bfloat16 [768, 1536], P('row', 'col'), may hold values from -0.21875 to 0.21875
- proj_inner: bfloat16 [768, 1536], P('row', 'col'), may hold values from -0.21875 to 0.21875
- proj_states: bfloat16 [768, 256], P('row'), may hold values from -0.21875 to 0.21875
- proj_step: bfloat16 [768, 24], P('row', 'col'), may hold values from -0.21875 to 0.21875
- conv_inner_weight: float32 [4, 1536], P(None, 'col'), may hold values from -3 to 3
- conv_inner_bias: float32 [1536], P('col'), may hold values from -3 to 3
- conv_state_weight: float32 [4, 256], replicated, may hold values from -3 to 3
- conv_state_bias: float32 [256], replicated, may hold values from -3 to 3
- step_bias: float32 [24], P('col'), may hold values from -6 to -2.5
- decay_log: float32 [24], P('col'), may hold values from 0 to 2.77
- skip_gain: float32 [24], P('col'), may hold values from 0.5 to 1.5
- gated_gain: float32 [1536], P('col'), may hold values from 0.5 to 1.5
- proj_out: bfloat16 [1536, 768], P('col', 'row'), may hold values from -0.15625 to 0.15625
- out_grad: bfloat16 [32768, 768], P(('dp', 'row'), 'col'), may hold values from -6 to 6
Outputs:
- block_out: bfloat16 [32768, 768], P(('dp', 'row'), 'col')
- grad_hidden: float32 [32768, 768], P(('dp', 'row'), 'col')
- grad_norm_gain: float32 [768], P('col')
- grad_proj_gate: float32 [768, 1536], P('row', 'col')
- grad_proj_inner: float32 [768, 1536], P('row', 'col')
- grad_proj_states: float32 [768, 256], P('row')
- grad_proj_step: float32 [768, 24], P('row', 'col')
- grad_conv_inner_weight: float32 [4, 1536], P(None, 'col')
- grad_conv_inner_bias: float32 [1536], P('col')
- grad_conv_state_weight: float32 [4, 256], replicated
- grad_conv_state_bias: float32 [256], replicated
- grad_step_bias: float32 [24], P('col')
- grad_decay_log: float32 [24], P('col')
- grad_skip_gain: float32 [24], P('col')
- grad_gated_gain: float32 [1536], P('col')
- grad_proj_out: float32 [1536, 768], P('col', 'row')
The draws below stay inside these ranges and needn't reach their ends.
Inputs may be any that keep to these rules, and one draw needn't show every extreme that they name: `doc_ids`: along each pack the numbers never fall, and each run of one number is 1 to 1024 tokens long.
All inputs are finite; a program needn't handle non-finite values.
Results may differ from the reference program's by a relative error of at most 0.012.
Values may be sent and summed in bfloat16 or wider, within the bound.
A program may use at most 192 MiB of HBM per device.

```python
import math
import jax
import jax.numpy as jnp
import numpy as np
from jax import lax

D = 768
H = 24
N = 128
KW = 4
DI = 1536
BLOCK = 256
SEGS = 4
TOK_DEV = 2048
PACKS = 16
TOKENS = 32768


def shard_levels(own_key, shape, shards, least, top_value):
    level, own = 1.0, jax.random.fold_in(own_key, 6)
    for dim, parts in shards:
        heights = jnp.exp(jax.random.uniform(jax.random.fold_in(own, dim), (parts,), jnp.float32, least / len(shards), top_value / len(shards)))
        level = level * jnp.repeat(heights, shape[dim] // parts).reshape([-1 if axis == dim else 1 for axis in range(len(shape))])
    return level


def split_up(amount, total, reach, slope):
    weights = [(1 << 20) // math.isqrt(rank ** slope) + 1 for rank in range(2, amount + 1)]
    surplus, given = total - reach - (amount - 1), [1] * (amount - 1)
    while surplus > 0:
        candidates = [i for i in range(amount - 1) if given[i] < reach]
        mass, left = sum([weights[i] for i in candidates]), surplus
        for i in candidates:
            extra = min(reach - given[i], max(1, left * weights[i] // mass), surplus)
            given[i] = given[i] + extra
            surplus = surplus - extra
    return np.array([reach] + given)


def ragged(key, count, total, reach, lean):
    if count == 2:
        one = jax.random.randint(key, (), max(1, total - reach), min(reach, total - 1) + 1)
        return jnp.stack([one, total - one])
    lengths = jnp.asarray(split_up(count, total, reach, lean), jnp.int32)
    couples = (count - 1) // 2
    giver, receiver = lengths[1:1 + 2 * couples:2], lengths[2:2 + 2 * couples:2]
    slack = jnp.minimum(giver - 1, reach - receiver)
    moved = jax.random.randint(jax.random.fold_in(key, 1), (couples,), 0, 1 << 20) % (slack + 1)
    lengths = lengths.at[1:1 + 2 * couples:2].set(giver - moved).at[2:2 + 2 * couples:2].set(receiver + moved)
    return lengths[jax.random.permutation(jax.random.fold_in(key, 2), count)]


def scatter_about(key, extent, scale, most, split=(), kind=jnp.bfloat16):
    gain = shard_levels(key, extent, split, -0.22, 0.18) if split else 1.0
    values = jax.random.normal(key, extent, jnp.float32) * scale * gain
    return jnp.minimum(jnp.maximum(values, -most), most).astype(kind)


def setup_inputs(seed: int = 0) -> dict:
    key_list = jax.random.split(jax.random.key(seed), 18)
    return {
        "hidden_in": scatter_about(key_list[0], (TOKENS, D), 1.0, 6.0, ((0, 16), (1, 2))),
        "doc_ids": jax.vmap(lambda own: jnp.searchsorted(jnp.cumsum(ragged(own, SEGS, TOK_DEV, TOK_DEV // 2, 0)), jnp.arange(TOK_DEV), side="right"))(jax.random.split(key_list[1], PACKS)).reshape((PACKS, TOK_DEV)).astype(jnp.int32),
        "norm_gain": jnp.clip(1.0 + 0.1 * jax.random.normal(key_list[2], (D,), jnp.float32), 0.5, 1.5).astype(jnp.bfloat16),
        "proj_gate": scatter_about(key_list[3], (D, DI), D ** -0.5, 0.21875, ((0, 4), (1, 2))),
        "proj_inner": scatter_about(key_list[4], (D, DI), D ** -0.5, 0.21875, ((0, 4), (1, 2))),
        "proj_states": scatter_about(key_list[5], (D, 2 * N), D ** -0.5, 0.21875, ((0, 4),)),
        "proj_step": scatter_about(key_list[6], (D, H), D ** -0.5, 0.21875, ((0, 4), (1, 2))),
        "conv_inner_weight": scatter_about(key_list[7], (KW, DI), KW ** -0.5, 3.0, ((1, 2),), jnp.float32),
        "conv_inner_bias": scatter_about(key_list[8], (DI,), 0.5, 3.0, ((0, 2),), jnp.float32),
        "conv_state_weight": scatter_about(key_list[9], (KW, 2 * N), KW ** -0.5, 3.0, (), jnp.float32),
        "conv_state_bias": scatter_about(key_list[10], (2 * N,), 0.5, 3.0, (), jnp.float32),
        "step_bias": jnp.clip(-6.0 + 3.5 * jax.random.uniform(key_list[11], (H,), jnp.float32) ** shard_levels(key_list[11], (H,), ((0, 2),), -0.2, 0.2), -6.0, -2.5),
        "decay_log": jnp.clip(2.77 * jax.random.uniform(key_list[12], (H,), jnp.float32) ** shard_levels(key_list[12], (H,), ((0, 2),), -0.2, 0.2), 0.0, 2.77),
        "skip_gain": jnp.clip(0.5 + 1.0 * jax.random.uniform(key_list[13], (H,), jnp.float32) ** shard_levels(key_list[13], (H,), ((0, 2),), -0.2, 0.2), 0.5, 1.5),
        "gated_gain": jnp.clip(1.0 + 0.1 * jax.random.normal(key_list[14], (DI,), jnp.float32), 0.5, 1.5),
        "proj_out": scatter_about(key_list[15], (DI, D), DI ** -0.5, 0.15625, ((0, 2), (1, 4))),
        "out_grad": scatter_about(key_list[16], (TOKENS, D), 1.0, 6.0, ((0, 16), (1, 2))),
    }


epsilon = 1e-05
highest = lax.Precision.HIGHEST

@jax.custom_vjp
def low(v):
    return lax.optimization_barrier(v.astype(jnp.bfloat16)).astype(jnp.float32)

@jax.custom_vjp
def low_back(v):
    return v

def low_keep(v):
    return (low(v), None)

def low_pass(kept, grad):
    return (grad,)

def back_keep(v):
    return (v, None)

def back_low(kept, grad):
    return (low(grad),)
low.defvjp(low_keep, low_pass)
low_back.defvjp(back_keep, back_low)

def shift_masks(doc_row):
    rows_list = [jnp.ones(doc_row.shape, jnp.float32)]
    for offset in range(1, KW):
        earlier = jnp.concatenate([jnp.full((offset,), -1, jnp.int32), doc_row[:-offset]])
        rows_list.append((earlier == doc_row).astype(jnp.float32))
    return jnp.stack(rows_list)

def conv_mix(values, weight, bias_row, near_masks):
    taps = weight.shape[0]
    conv_sum = bias_row[None, :] + weight[taps - 1][None, :] * values
    for offset in range(1, taps):
        pad_rows = jnp.zeros((offset, values.shape[1]), jnp.float32)
        shifted = jnp.concatenate([pad_rows, values[:-offset]], axis=0)
        conv_sum = conv_sum + weight[taps - 1 - offset][None, :] * shifted * near_masks[offset][:, None]
    return jax.nn.silu(conv_sum)

def ssd_scan(inner_vals, write_vec, read_vec, log_rate, step_size, doc_row, skip_gain):
    tokens, head_count, head_dim = inner_vals.shape
    blocks = tokens // BLOCK
    rate_heads = jnp.transpose(log_rate.reshape(blocks, BLOCK, head_count), (0, 2, 1))
    step_heads = jnp.transpose(step_size.reshape(blocks, BLOCK, head_count), (0, 2, 1))
    pieces = (inner_vals.reshape(blocks, BLOCK, head_count, head_dim), write_vec.reshape(blocks, BLOCK, -1), read_vec.reshape(blocks, BLOCK, -1), rate_heads, step_heads, doc_row.reshape(blocks, BLOCK))
    positions = jnp.arange(BLOCK)
    lower_tri = positions[:, None] >= positions[None, :]

    def one_block(carry_in, block_data):
        carried, last_doc = carry_in
        inner_blk, write_blk, read_blk, rate_blk, step_blk, doc_blk = block_data
        cumulative = jnp.cumsum(rate_blk, axis=1)
        allowed = lower_tri & (doc_blk[:, None] == doc_blk[None, :])
        allowed_wide = allowed[None, :, :]
        log_gaps = cumulative[:, :, None] - cumulative[:, None, :]
        decay_mat = jnp.exp(jnp.where(allowed_wide, log_gaps, 0.0)) * allowed_wide.astype(jnp.float32)
        scores = jnp.dot(read_blk, write_blk.T, precision=highest)
        mixing = scores[None, :, :] * decay_mat * step_blk[:, None, :]
        local_out = jnp.einsum('hts,shp->thp', mixing, inner_blk, precision=highest)
        enter_scale = (doc_blk == last_doc).astype(jnp.float32)[None, :] * jnp.exp(cumulative)
        from_state = jnp.einsum('tn,hpn->thp', read_blk, carried, precision=highest) * enter_scale.T[:, :, None]
        result = local_out + from_state + skip_gain[None, :, None] * inner_blk
        final_doc = doc_blk[BLOCK - 1]
        keep_state = (final_doc == last_doc).astype(jnp.float32)
        weights_tail = jnp.exp(cumulative[:, BLOCK - 1:] - cumulative) * step_blk * (doc_blk == final_doc).astype(jnp.float32)[None, :]
        update = jnp.einsum('hs,shp,sn->hpn', weights_tail, inner_blk, write_blk, precision=highest)
        carried = keep_state * jnp.exp(cumulative[:, BLOCK - 1])[:, None, None] * carried + update
        return ((carried, final_doc), result)
    start_carry = (jnp.zeros((head_count, head_dim, write_vec.shape[1]), jnp.float32), jnp.array(-1, jnp.int32))
    final_carry, outputs = lax.scan(jax.checkpoint(one_block), start_carry, pieces)
    return outputs.reshape(tokens, head_count, head_dim)

def mixer_core(near_masks, doc_row, gate_in, inner_in, state_in, step_in, conv_inner_weight, conv_inner_bias, conv_state_weight, conv_state_bias, step_bias, decay_log, skip_gain):
    tokens = gate_in.shape[0]
    head_count = step_in.shape[1]
    states = state_in.shape[1] // 2
    inner_vals = low(conv_mix(inner_in, conv_inner_weight, conv_inner_bias, near_masks))
    state_vals = low(conv_mix(state_in, conv_state_weight, conv_state_bias, near_masks))
    step_size = jax.nn.softplus(step_in + step_bias[None, :])
    log_rate = -jnp.exp(decay_log)[None, :] * step_size
    mixed_out = ssd_scan(inner_vals.reshape(tokens, head_count, -1), state_vals[:, :states], state_vals[:, states:], log_rate, step_size, doc_row, skip_gain)
    return mixed_out.reshape(tokens, -1) * jax.nn.silu(gate_in)

def pack_forward(params, hidden, doc_row):
    norm_gain, proj_gate, proj_inner, proj_states, proj_step, conv_inner_weight, conv_inner_bias, conv_state_weight, conv_state_bias, step_bias, decay_log, skip_gain, gated_gain, proj_out = params
    inv_in = lax.rsqrt(lax.optimization_barrier(jnp.mean(hidden * hidden, axis=1, keepdims=True)) + epsilon)
    normed = low(hidden * inv_in * norm_gain[None, :])
    gate_in = low_back(jnp.dot(normed, proj_gate, precision=highest))
    inner_in = low_back(jnp.dot(normed, proj_inner, precision=highest))
    state_in = jnp.dot(normed, proj_states, precision=highest)
    step_in = low_back(jnp.dot(normed, proj_step, precision=highest))
    near_masks = shift_masks(doc_row)
    gated_vals = mixer_core(near_masks, doc_row, gate_in, inner_in, state_in, step_in, conv_inner_weight, conv_inner_bias, conv_state_weight, conv_state_bias, step_bias, decay_log, skip_gain)
    inv_gated = lax.rsqrt(lax.optimization_barrier(jnp.mean(gated_vals * gated_vals, axis=1, keepdims=True)) + epsilon)
    normed_out = low(gated_vals * inv_gated * gated_gain[None, :])
    return hidden + jnp.dot(normed_out, proj_out, precision=highest)

def reference(hidden_in, doc_ids, norm_gain, proj_gate, proj_inner, proj_states, proj_step, conv_inner_weight, conv_inner_bias, conv_state_weight, conv_state_bias, step_bias, decay_log, skip_gain, gated_gain, proj_out, out_grad):
    params = (norm_gain.astype(jnp.float32), proj_gate.astype(jnp.float32), proj_inner.astype(jnp.float32), proj_states.astype(jnp.float32), proj_step.astype(jnp.float32), conv_inner_weight.astype(jnp.float32), conv_inner_bias.astype(jnp.float32), conv_state_weight.astype(jnp.float32), conv_state_bias.astype(jnp.float32), step_bias.astype(jnp.float32), decay_log.astype(jnp.float32), skip_gain.astype(jnp.float32), gated_gain.astype(jnp.float32), proj_out.astype(jnp.float32))
    packed = hidden_in.astype(jnp.float32).reshape(PACKS, TOK_DEV, D)

    def forward(packed_in, params_in):

        def one_pack(pack_item):
            return pack_forward(params_in, pack_item[0], pack_item[1])
        return lax.map(jax.checkpoint(one_pack), (packed_in, doc_ids))
    outputs, pullback = jax.vjp(forward, packed, params)
    grad_packed, grad_list = pullback(out_grad.astype(jnp.float32).reshape(PACKS, TOK_DEV, D))
    return (outputs.reshape(TOKENS, D).astype(jnp.bfloat16), grad_packed.reshape(TOKENS, D), grad_list[0], grad_list[1], grad_list[2], grad_list[3], grad_list[4], grad_list[5], grad_list[6], grad_list[7], grad_list[8], grad_list[9], grad_list[10], grad_list[11], grad_list[12], grad_list[13])
```

```python
from functools import partial

import jax
import jax.numpy as jnp
import numpy as np
from jax import lax
from jax.experimental import pallas as pl
from jax.experimental.pallas import tpu as pltpu
from jax.sharding import PartitionSpec as P

KW = 4
BLOCK = 256


epsilon = 1e-05
highest = lax.Precision.HIGHEST
INTERPRET = False


def round_keep(values):
    rounded = values.astype(jnp.bfloat16).astype(jnp.float32)
    return values + lax.stop_gradient(rounded - values)


def shift_masks(doc_row):
    rows_list = [jnp.ones(doc_row.shape, jnp.float32)]
    for offset in range(1, KW):
        earlier = jnp.concatenate([jnp.full((offset,), -1, jnp.int32), doc_row[:-offset]])
        rows_list.append((earlier == doc_row).astype(jnp.float32))
    return jnp.stack(rows_list)


def conv_mix(values, weight, bias_row, near_masks):
    taps = weight.shape[0]
    conv_sum = bias_row[None, :] + weight[taps - 1][None, :] * values
    for offset in range(1, taps):
        pad_rows = jnp.zeros((offset, values.shape[1]), jnp.float32)
        shifted = jnp.concatenate([pad_rows, values[:-offset]], axis=0)
        conv_sum = (
            conv_sum + weight[taps - 1 - offset][None, :] * shifted * near_masks[offset][:, None]
        )
    return jax.nn.silu(conv_sum)


def dot_f32(left, right, dims=((1,), (0,))):
    return lax.dot_general(left, right, (dims, ((), ())), preferred_element_type=jnp.float32)


def pair_wide(columns, pair, low_lanes):
    first = columns[:, 2 * pair : 2 * pair + 1]
    second = columns[:, 2 * pair + 1 : 2 * pair + 2]
    return jnp.where(low_lanes, first, second)


def decay_of(cum, cum_rows, head, bias):
    return jnp.exp(cum[:, head : head + 1] - cum_rows[head : head + 1, :] + bias)


def mask_bias(doc_col, doc_line):
    size = doc_col.shape[0]
    later = lax.broadcasted_iota(jnp.int32, (size, size), 0)
    earlier = lax.broadcasted_iota(jnp.int32, (size, size), 1)
    return jnp.where((later >= earlier) & (doc_col == doc_line), 0.0, -1e30)


def scan_forward_kernel(
    inner_ref, write_ref, read_ref, cum_ref, cumrow_ref, enter_ref, tail_ref, step_ref,
    doccol_ref, docrow_ref, out_ref, state_ref, carried,
):
    @pl.when(pl.program_id(0) == 0)
    def _():
        carried[...] = jnp.zeros(carried.shape, jnp.float32)

    write, read = write_ref[...], read_ref[...]
    cum, cum_rows = cum_ref[...], cumrow_ref[...]
    enter, tail, step = enter_ref[...], tail_ref[...], step_ref[...]
    size, width = inner_ref.shape
    pair_lanes = 2 * width // cum.shape[1]
    low_lanes = lax.broadcasted_iota(jnp.int32, (1, pair_lanes), 1) < pair_lanes // 2
    bias = mask_bias(doccol_ref[...], docrow_ref[...])
    scores = dot_f32(read, write, ((1,), (1,)))
    for pair in range(width // pair_lanes):
        cols = slice(pair * pair_lanes, (pair + 1) * pair_lanes)
        stepped = inner_ref[:, cols].astype(jnp.float32) * pair_wide(step, pair, low_lanes)
        scaled = stepped.astype(jnp.bfloat16)
        mix_a = (scores * decay_of(cum, cum_rows, 2 * pair, bias)).astype(jnp.bfloat16)
        mix_b = (scores * decay_of(cum, cum_rows, 2 * pair + 1, bias)).astype(jnp.bfloat16)
        local = jnp.where(low_lanes, dot_f32(mix_a, scaled), dot_f32(mix_b, scaled))
        state = carried[:, cols]
        state_ref[0, :, cols] = state
        enter_wide = pair_wide(enter, pair, low_lanes)
        out_ref[:, cols] = local + enter_wide * dot_f32(read, state.astype(jnp.bfloat16))
        weighted = (scaled.astype(jnp.float32) * pair_wide(tail, pair, low_lanes)).astype(
            jnp.bfloat16
        )
        carried[:, cols] = enter_wide[size - 1 : size, :] * state + dot_f32(
            write, weighted, ((0,), (0,))
        )


def scan_backward_kernel(
    inner_ref, write_ref, read_ref, cum_ref, cumrow_ref, enter_ref, tail_ref, step_ref,
    doccol_ref, docrow_ref, out_ref, state_ref, grad_ref,
    dinner_ref, dwrite_ref, dread_ref, dcum_ref, dstep_ref, carried,
):
    @pl.when(pl.program_id(0) == 0)
    def _():
        carried[...] = jnp.zeros(carried.shape, jnp.float32)

    write, read = write_ref[...], read_ref[...]
    cum, cum_rows = cum_ref[...], cumrow_ref[...]
    enter, tail, step = enter_ref[...], tail_ref[...], step_ref[...]
    size, width = inner_ref.shape
    heads = cum.shape[1]
    pair_lanes = 2 * width // heads
    low_lanes = lax.broadcasted_iota(jnp.int32, (1, pair_lanes), 1) < pair_lanes // 2
    head_lane = lax.broadcasted_iota(jnp.int32, (1, heads), 1)
    last_row = lax.broadcasted_iota(jnp.int32, (size, 1), 0) == size - 1
    bias = mask_bias(doccol_ref[...], docrow_ref[...])
    scores = dot_f32(read, write, ((1,), (1,)))
    dscores = jnp.zeros((size, size), jnp.float32)
    dread = jnp.zeros(read.shape, jnp.float32)
    dwrite = jnp.zeros(write.shape, jnp.float32)
    dcum = jnp.zeros((size, heads), jnp.float32)
    dstep = jnp.zeros((size, heads), jnp.float32)
    for pair in range(width // pair_lanes):
        cols = slice(pair * pair_lanes, (pair + 1) * pair_lanes)
        step_wide = pair_wide(step, pair, low_lanes)
        inner = inner_ref[:, cols].astype(jnp.float32)
        scaled = (inner * step_wide).astype(jnp.bfloat16)
        scaled_f = scaled.astype(jnp.float32)
        grad = grad_ref[:, cols].astype(jnp.bfloat16)
        grad_f = grad.astype(jnp.float32)
        decay_a = decay_of(cum, cum_rows, 2 * pair, bias)
        decay_b = decay_of(cum, cum_rows, 2 * pair + 1, bias)
        mix_a = (scores * decay_a).astype(jnp.bfloat16)
        mix_b = (scores * decay_b).astype(jnp.bfloat16)
        local = jnp.where(
            low_lanes,
            dot_f32(mix_a, grad, ((0,), (0,))),
            dot_f32(mix_b, grad, ((0,), (0,))),
        )
        grad_a = jnp.where(low_lanes, grad_f, 0.0).astype(jnp.bfloat16)
        grad_b = jnp.where(low_lanes, 0.0, grad_f).astype(jnp.bfloat16)
        dscores = (
            dscores
            + dot_f32(grad_a, scaled, ((1,), (1,))) * decay_a
            + dot_f32(grad_b, scaled, ((1,), (1,))) * decay_b
        )
        state = state_ref[0, :, cols]
        dstate = carried[:, cols]
        dstate_low = dstate.astype(jnp.bfloat16)
        tail_wide = pair_wide(tail, pair, low_lanes)
        enter_wide = pair_wide(enter, pair, low_lanes)
        enter_end = enter_wide[size - 1 : size, :]
        from_tail = tail_wide * dot_f32(write, dstate_low)
        dscaled = local + from_tail
        entered = (enter_wide * grad_f).astype(jnp.bfloat16)
        weighted = (scaled_f * tail_wide).astype(jnp.bfloat16)
        dread = dread + dot_f32(entered, state.astype(jnp.bfloat16), ((1,), (1,)))
        dwrite = dwrite + dot_f32(weighted, dstate_low, ((1,), (1,)))
        carried[:, cols] = dot_f32(read, entered, ((0,), (0,))) + enter_end * dstate
        dinner_ref[:, cols] = dscaled * step_wide
        row_part = grad_f * out_ref[:, cols] - scaled_f * dscaled
        end_part = jnp.sum(scaled_f * from_tail, axis=0, keepdims=True) + enter_end * jnp.sum(
            dstate * state, axis=0, keepdims=True
        )
        row_part = row_part + jnp.where(last_row, end_part, 0.0)
        step_part = dscaled * inner
        for side in range(2):
            lanes = low_lanes if side == 0 else jnp.logical_not(low_lanes)
            own = head_lane == 2 * pair + side
            row_sum = jnp.sum(jnp.where(lanes, row_part, 0.0), axis=1, keepdims=True)
            step_sum = jnp.sum(jnp.where(lanes, step_part, 0.0), axis=1, keepdims=True)
            dcum = dcum + jnp.where(own, row_sum, 0.0)
            dstep = dstep + jnp.where(own, step_sum, 0.0)
    dscores_low = dscores.astype(jnp.bfloat16)
    dread_ref[...] = dread + dot_f32(dscores_low, write)
    dwrite_ref[...] = dwrite + dot_f32(dscores_low, read, ((0,), (0,)))
    dcum_ref[...] = dcum
    dstep_ref[...] = dstep


def scan_operands(inner_vals, write_vec, read_vec, log_rate, step_size, doc_row):
    tokens, heads = log_rate.shape
    blocks = tokens // BLOCK
    lower = jnp.tril(jnp.ones((BLOCK, BLOCK), jnp.float32))
    cum = jnp.einsum(
        "ts,bsh->bth", lower, log_rate.reshape(blocks, BLOCK, heads), precision=highest
    )
    doc_blocks = doc_row.reshape(blocks, BLOCK)
    final = doc_blocks[:, BLOCK - 1]
    before = jnp.concatenate([jnp.full((1,), -1, jnp.int32), final[:-1]])
    enter = (doc_blocks == before[:, None]).astype(jnp.float32)[:, :, None] * jnp.exp(cum)
    tail = (doc_blocks == final[:, None]).astype(jnp.float32)[:, :, None] * jnp.exp(
        cum[:, BLOCK - 1 :] - cum
    )
    flat_cum = cum.reshape(tokens, heads)
    return (
        inner_vals.astype(jnp.bfloat16),
        write_vec.astype(jnp.bfloat16),
        read_vec.astype(jnp.bfloat16),
        flat_cum,
        flat_cum.T,
        enter.reshape(tokens, heads),
        tail.reshape(tokens, heads),
        step_size,
        doc_row[:, None],
        doc_row[None, :],
    )


def scan_specs(width, states, heads, place):
    def rows(columns):
        return pl.BlockSpec((BLOCK, columns), lambda i: (place(i), 0))

    def lines(count):
        return pl.BlockSpec((count, BLOCK), lambda i: (0, place(i)))

    return [
        rows(width), rows(states), rows(states), rows(heads), lines(heads),
        rows(heads), rows(heads), rows(heads), rows(1), lines(1),
    ]


def scan_call(operands):
    tokens, width = operands[0].shape
    states, heads = operands[1].shape[1], operands[3].shape[1]
    blocks = tokens // BLOCK
    return pl.pallas_call(
        scan_forward_kernel,
        grid=(blocks,),
        in_specs=scan_specs(width, states, heads, lambda i: i),
        out_specs=[
            pl.BlockSpec((BLOCK, width), lambda i: (i, 0)),
            pl.BlockSpec((1, states, width), lambda i: (i, 0, 0)),
        ],
        out_shape=[
            jax.ShapeDtypeStruct((tokens, width), jnp.float32),
            jax.ShapeDtypeStruct((blocks, states, width), jnp.float32),
        ],
        scratch_shapes=[pltpu.VMEM((states, width), jnp.float32)],
        interpret=INTERPRET,
    )(*operands)


@jax.custom_vjp
def ssd_scan(inner_vals, write_vec, read_vec, log_rate, step_size, doc_row):
    return scan_call(scan_operands(inner_vals, write_vec, read_vec, log_rate, step_size, doc_row))[0]


def ssd_keep(*arguments):
    operands = scan_operands(*arguments)
    mixed, states_in = scan_call(operands)
    return mixed, (operands, mixed, states_in)


def ssd_back(kept, grad):
    operands, mixed, states_in = kept
    tokens, width = mixed.shape
    blocks, states, _ = states_in.shape
    heads = operands[3].shape[1]

    def place(i):
        return blocks - 1 - i

    def rows(columns):
        return pl.BlockSpec((BLOCK, columns), lambda i: (place(i), 0))

    dinner, dwrite, dread, dcum, dstep = pl.pallas_call(
        scan_backward_kernel,
        grid=(blocks,),
        in_specs=scan_specs(width, states, heads, place)
        + [rows(width), pl.BlockSpec((1, states, width), lambda i: (place(i), 0, 0)), rows(width)],
        out_specs=[rows(width), rows(states), rows(states), rows(heads), rows(heads)],
        out_shape=[
            jax.ShapeDtypeStruct((tokens, columns), jnp.float32)
            for columns in (width, states, states, heads, heads)
        ],
        scratch_shapes=[pltpu.VMEM((states, width), jnp.float32)],
        interpret=INTERPRET,
    )(*operands, mixed, states_in, grad)
    upper = jnp.triu(jnp.ones((BLOCK, BLOCK), jnp.float32))
    drate = jnp.einsum(
        "ut,bth->buh", upper, dcum.reshape(blocks, BLOCK, heads), precision=highest
    ).reshape(tokens, heads)
    return dinner, dwrite, dread, drate, dstep, np.zeros((tokens,), jax.dtypes.float0)


ssd_scan.defvjp(ssd_keep, ssd_back)


def mixer_core(
    near_masks,
    doc_row,
    gate_in,
    inner_in,
    state_in,
    step_in,
    conv_inner_weight,
    conv_inner_bias,
    conv_state_weight,
    conv_state_bias,
    step_bias,
    decay_log,
    skip_gain,
):
    tokens = gate_in.shape[0]
    head_count = step_in.shape[1]
    states = state_in.shape[1] // 2
    inner_vals = round_keep(conv_mix(inner_in, conv_inner_weight, conv_inner_bias, near_masks))
    state_vals = round_keep(conv_mix(state_in, conv_state_weight, conv_state_bias, near_masks))
    step_size = jax.nn.softplus(step_in + step_bias[None, :])
    log_rate = -jnp.exp(decay_log)[None, :] * step_size
    mixed_out = ssd_scan(
        inner_vals,
        state_vals[:, :states],
        state_vals[:, states:],
        log_rate,
        step_size,
        doc_row,
    )
    head_dim = inner_vals.shape[1] // head_count
    mixed_out = mixed_out + jnp.repeat(skip_gain, head_dim)[None, :] * inner_vals
    return mixed_out * jax.nn.silu(gate_in)


def pack(arrays):
    return jnp.concatenate([array.reshape(-1) for array in arrays])


def unpack(flat, arrays):
    results, start = [], 0
    for array in arrays:
        results.append(flat[start : start + array.size].reshape(array.shape))
        start += array.size
    return results


def body(
    hidden_in,
    doc_ids,
    norm_gain,
    proj_gate,
    proj_inner,
    proj_states,
    proj_step,
    conv_inner_weight,
    conv_inner_bias,
    conv_state_weight,
    conv_state_bias,
    step_bias,
    decay_log,
    skip_gain,
    gated_gain,
    proj_out,
    out_grad,
):
    doc_row = doc_ids[0]
    full_hidden, full_grad, full_gain = (
        lax.all_gather(hidden_in, "col", axis=1, tiled=True),
        lax.all_gather(out_grad, "col", axis=1, tiled=True),
        lax.all_gather(norm_gain, "col", axis=0, tiled=True),
    )
    gate_all, inner_all, states_all, step_all, out_all = (
        lax.all_gather(proj_gate, "row", axis=0, tiled=True),
        lax.all_gather(proj_inner, "row", axis=0, tiled=True),
        lax.all_gather(proj_states, "row", axis=0, tiled=True),
        lax.all_gather(proj_step, "row", axis=0, tiled=True),
        lax.all_gather(proj_out, "row", axis=1, tiled=True),
    )
    model_width = full_hidden.shape[1]
    hidden_float = full_hidden.astype(jnp.float32)
    inv_in = lax.rsqrt(jnp.mean(hidden_float * hidden_float, axis=1, keepdims=True) + epsilon)
    normed = (hidden_float * inv_in * full_gain.astype(jnp.float32)[None, :]).astype(jnp.bfloat16)
    gate_in = jnp.dot(normed, gate_all, preferred_element_type=jnp.float32)
    inner_in = jnp.dot(normed, inner_all, preferred_element_type=jnp.float32)
    state_in = jnp.dot(normed, states_all, preferred_element_type=jnp.float32)
    step_in = jnp.dot(normed, step_all, preferred_element_type=jnp.float32)
    near_masks = shift_masks(doc_row)
    mixer_local = partial(mixer_core, near_masks, doc_row)
    gated_vals, core_back = jax.vjp(
        mixer_local,
        gate_in,
        inner_in,
        state_in,
        step_in,
        conv_inner_weight,
        conv_inner_bias,
        conv_state_weight,
        conv_state_bias,
        step_bias,
        decay_log,
        skip_gain,
    )
    inner_width = gated_vals.shape[1] * lax.axis_size("col")
    gated_sq = lax.psum(jnp.sum(gated_vals * gated_vals, axis=1), "col")
    inv_gated = lax.rsqrt(gated_sq / inner_width + epsilon)[:, None]
    hat_gated = gated_vals * inv_gated
    normed_out = (hat_gated * gated_gain[None, :]).astype(jnp.bfloat16)
    out_part = jnp.dot(normed_out, out_all, preferred_element_type=jnp.float32)
    out_share = lax.psum_scatter(out_part, "col", scatter_dimension=1, tiled=True)
    block_out = (hidden_in.astype(jnp.float32) + out_share).astype(jnp.bfloat16)
    grad_out_full = jnp.einsum(
        "ti,td->di", normed_out, full_grad, preferred_element_type=jnp.float32
    )
    out_summed = lax.psum(
        lax.psum_scatter(
            grad_out_full.astype(jnp.bfloat16), "row", scatter_dimension=0, tiled=True
        ),
        "dp",
    )
    grad_normed_out = jnp.einsum(
        "td,id->ti", full_grad, out_all, preferred_element_type=jnp.float32
    )
    scaled_out = grad_normed_out * gated_gain[None, :]
    grad_gated_gain = jnp.sum(grad_normed_out * hat_gated, axis=0)
    dot_gated = lax.psum(jnp.sum(scaled_out * hat_gated, axis=1), "col")
    grad_gated = inv_gated * (scaled_out - hat_gated * (dot_gated / inner_width)[:, None])
    (
        grad_gate,
        grad_inner,
        grad_state,
        grad_step,
        grad_conv_inner_weight,
        grad_conv_inner_bias,
        grad_conv_state_weight,
        grad_conv_state_bias,
        grad_step_bias,
        grad_decay_log,
        grad_skip_gain,
    ) = core_back(grad_gated)
    gate_back = grad_gate.astype(jnp.bfloat16)
    inner_back = grad_inner.astype(jnp.bfloat16)
    step_back = grad_step.astype(jnp.bfloat16)
    state_back = grad_state.astype(jnp.bfloat16)
    grad_gate_full = jnp.einsum("td,tf->df", normed, gate_back, preferred_element_type=jnp.float32)
    grad_inner_full = jnp.einsum(
        "td,tf->df", normed, inner_back, preferred_element_type=jnp.float32
    )
    grad_step_full = jnp.einsum("td,tf->df", normed, step_back, preferred_element_type=jnp.float32)
    grad_states_full = jnp.einsum(
        "td,tf->df", normed, state_back, preferred_element_type=jnp.float32
    )
    grad_normed = jnp.einsum("tf,df->td", gate_back, gate_all, preferred_element_type=jnp.float32)
    grad_normed = grad_normed + jnp.einsum(
        "tf,df->td", inner_back, inner_all, preferred_element_type=jnp.float32
    )
    grad_normed = grad_normed + jnp.einsum(
        "tf,df->td", step_back, step_all, preferred_element_type=jnp.float32
    )
    grad_normed = grad_normed + jnp.einsum(
        "tf,df->td", state_back, states_all, preferred_element_type=jnp.float32
    )
    grad_share = lax.psum_scatter(grad_normed, "col", scatter_dimension=1, tiled=True)
    hat_own = hidden_in.astype(jnp.float32) * inv_in
    scaled_in = grad_share * norm_gain.astype(jnp.float32)[None, :]
    grad_norm_gain = jnp.sum(grad_share * hat_own, axis=0)
    dot_in = lax.psum(jnp.sum(scaled_in * hat_own, axis=1), "col")
    grad_hidden = out_grad.astype(jnp.float32) + inv_in * (
        scaled_in - hat_own * (dot_in / model_width)[:, None]
    )
    wide = jnp.concatenate(
        [grad_gate_full, grad_inner_full, grad_states_full, grad_step_full], axis=1
    ).astype(jnp.bfloat16)
    wide = lax.psum_scatter(wide, "row", scatter_dimension=0, tiled=True)
    wide = lax.psum(wide, "dp").astype(jnp.float32)
    gate_cols, inner_cols = proj_gate.shape[1], proj_inner.shape[1]
    state_cols = proj_states.shape[1]
    first, second = gate_cols + inner_cols, gate_cols + inner_cols + state_cols
    smalls_own = (
        grad_norm_gain,
        grad_conv_inner_weight,
        grad_conv_inner_bias,
        grad_step_bias,
        grad_decay_log,
        grad_skip_gain,
        grad_gated_gain,
    )
    own = unpack(lax.psum(pack(smalls_own), ("dp", "row")), smalls_own)
    smalls_all = (grad_conv_state_weight, grad_conv_state_bias)
    shared = unpack(lax.psum(pack(smalls_all), ("dp", "row", "col")), smalls_all)
    return (
        block_out,
        grad_hidden,
        own[0],
        wide[:, :gate_cols],
        wide[:, gate_cols:first],
        lax.psum(wide[:, first:second], "col"),
        wide[:, second:],
        own[1],
        own[2],
        shared[0],
        shared[1],
        own[3],
        own[4],
        own[5],
        own[6],
        out_summed.astype(jnp.float32).T,
    )


def solution(mesh):
    in_specs = (
        P(("dp", "row"), "col"),
        P(("dp", "row"), None),
        P("col"),
        P("row", "col"),
        P("row", "col"),
        P("row", None),
        P("row", "col"),
        P(None, "col"),
        P("col"),
        P(),
        P(),
        P("col"),
        P("col"),
        P("col"),
        P("col"),
        P("col", "row"),
        P(("dp", "row"), "col"),
    )
    out_specs = (
        P(("dp", "row"), "col"),
        P(("dp", "row"), "col"),
        P("col"),
        P("row", "col"),
        P("row", "col"),
        P("row", None),
        P("row", "col"),
        P(None, "col"),
        P("col"),
        P(),
        P(),
        P("col"),
        P("col"),
        P("col"),
        P("col"),
        P("col", "row"),
    )
    return jax.shard_map(body, mesh=mesh, in_specs=in_specs, out_specs=out_specs, check_vma=False)
```
